32 devices in a mesh: ctx: 4 (over z), head: 8 (over y, x, core).
Axes of the slice: x: 2, y: 2, z: 4, core: 2. Of those that a mesh axis runs over, the one named last changes fastest.
Arguments:
- inputs: bfloat16 [8, 64, 4096], P('head', None, 'ctx'), may hold values from -6 to 6
- dt: float32 [8, 4096], P('head', 'ctx'), may hold values from 0.03 to 0.3
- decay_rate: float32 [8], P('head'), may hold values from 0.0024414062 to 0.4, as said below
- skip: float32 [8], P('head'), may hold values from 0.5 to 1.5
- b_proj: bfloat16 [128, 4096], P(None, 'ctx'), may hold values from -1.1953125 to 1.1953125
- c_proj: bfloat16 [128, 4096], P(None, 'ctx'), may hold values from -1.1953125 to 1.1953125
- lengths: int32 [16], replicated, may hold values from 1 to 1024, 4096 in all
- grad_out: bfloat16 [8, 64, 4096], P('head', None, 'ctx'), may hold values from -0.59765625 to 0.59765625
Outputs:
- mixed: bfloat16 [8, 64, 4096], P('head', None, 'ctx')
- grad_inputs: bfloat16 [8, 64, 4096], P('head', None, 'ctx')
- grad_dt: float32 [8, 4096], P('head', 'ctx')
- grad_b: float32 [128, 4096], P('head', 'ctx')
- grad_c: float32 [128, 4096], P('head', 'ctx')
The draws below stay inside these ranges and needn't reach their ends.
Inputs may be any that keep to these rules, and one draw needn't show every extreme that they name: `decay_rate`: each head's decay rate is positive.
All inputs are finite; a program needn't handle non-finite values.
Results may differ from the reference program's by a relative error of at most 0.001.
Values sent between devices are 32-bit elements; how exact they have to be, the bound alone decides.
A program may use at most 64 MiB of HBM per device.

```python
import math
import jax
import jax.numpy as jnp
import numpy as np
from jax import lax

P_SIZE = 64
N = 128
BLOCK = 128
NDOC = 16
HEADS = 8
SEQ = 4096
DOC_MOST = 1024


def draw_decay_rate(key, part):
    key_slow, key_fast, key_pick = jax.random.split(key, 3)
    slow_rate = jnp.exp(jax.random.uniform(key_slow, (HEADS,), jnp.float32, jnp.log(10.0 / SEQ), jnp.log(60.0 / SEQ)))
    fast_rate = jnp.exp(jax.random.uniform(key_fast, (HEADS,), jnp.float32, jnp.log(0.1), jnp.log(0.4)))
    picked = jax.random.randint(key_pick, (HEADS,), 0, 2) == 1
    return jnp.where(picked, slow_rate, fast_rate).astype(jnp.float32)


def shard_levels(stream_key, shape, shards, low, largest):
    level, own = 1.0, jax.random.fold_in(stream_key, 6)
    for dim, parts in shards:
        draws = jnp.exp(jax.random.uniform(jax.random.fold_in(own, dim), (parts,), jnp.float32, low / len(shards), largest / len(shards)))
        level = level * jnp.repeat(draws, shape[dim] // parts).reshape([-1 if axis == dim else 1 for axis in range(len(shape))])
    return level


def split_up(number_of, total, limit, slope):
    weights = [(1 << 20) // math.isqrt(grade ** slope) + 1 for grade in range(2, number_of + 1)]
    surplus, holding = total - limit - (number_of - 1), [1] * (number_of - 1)
    while surplus > 0:
        candidates = [i for i in range(number_of - 1) if holding[i] < limit]
        mass, budget = sum([weights[i] for i in candidates]), surplus
        for i in candidates:
            extra = min(limit - holding[i], max(1, budget * weights[i] // mass), surplus)
            holding[i] = holding[i] + extra
            surplus = surplus - extra
    return np.array([limit] + holding)


def ragged_sizes(own_key, amount, total, bound, slope):
    if amount == 2:
        one = jax.random.randint(own_key, (), max(1, total - bound), min(bound, total - 1) + 1)
        return jnp.stack([one, total - one])
    sizes = jnp.asarray(split_up(amount, total, bound, slope), jnp.int32)
    pairs = (amount - 1) // 2
    giver, receiver = sizes[1:1 + 2 * pairs:2], sizes[2:2 + 2 * pairs:2]
    room = jnp.minimum(giver - 1, bound - receiver)
    moved = jax.random.randint(jax.random.fold_in(own_key, 1), (pairs,), 0, 1 << 20) % (room + 1)
    sizes = sizes.at[1:1 + 2 * pairs:2].set(giver - moved).at[2:2 + 2 * pairs:2].set(receiver + moved)
    return sizes[jax.random.permutation(jax.random.fold_in(own_key, 2), amount)]


def noise(own_key, dims, spread, most, cuts=(), held_as=jnp.bfloat16):
    loudness = shard_levels(own_key, dims, cuts, -0.22, 0.18) if cuts else 1.0
    entries = jax.random.normal(own_key, dims, jnp.float32) * spread * loudness
    return jnp.minimum(jnp.maximum(entries, -most), most).astype(held_as)


def setup_inputs(seed: int = 0) -> dict:
    keys = jax.random.split(jax.random.key(seed), 9)
    inputs = noise(keys[0], (HEADS, P_SIZE, SEQ), 1.0, 6.0, ((0, 8), (2, 4)))
    dt = jnp.clip(jnp.exp(math.log(0.3) - 2.3025852 * jax.random.uniform(keys[1], (HEADS, SEQ), jnp.float32) ** shard_levels(keys[1], (HEADS, SEQ), ((0, 8), (1, 4)), -0.2, 0.2)), 0.03, 0.3)
    decay_rate = draw_decay_rate(jax.random.fold_in(keys[8], 71), 0)
    skip = jnp.clip(0.5 + 1.0 * jax.random.uniform(keys[3], (HEADS,), jnp.float32) ** shard_levels(keys[3], (HEADS,), ((0, 8),), -0.2, 0.2), 0.5, 1.5)
    b_proj = noise(keys[4], (N, SEQ), 0.2, 1.1953125, ((1, 4),))
    c_proj = noise(keys[5], (N, SEQ), 0.2, 1.1953125, ((1, 4),))
    lengths = ragged_sizes(keys[6], NDOC, SEQ, DOC_MOST, 2).astype(jnp.int32)
    grad_out = noise(keys[7], (HEADS, P_SIZE, SEQ), 0.1, 0.59765625, ((0, 8), (2, 4)))
    return {"inputs": inputs, "dt": dt, "decay_rate": decay_rate, "skip": skip, "b_proj": b_proj, "c_proj": c_proj, "lengths": lengths, "grad_out": grad_out}


HIGH = lax.Precision.HIGHEST

def mixing_block(state_in, block_data, decay_rate, skip_gain, lower_ones):
    x_block, dt_block, b_block, c_block, seg_block, prev_seg = block_data
    log_decay = -decay_rate * dt_block
    cumulative = jnp.dot(lower_ones, log_decay, precision=HIGH)
    pair_mask = (seg_block[:, None] == seg_block[None, :]) & (lower_ones > 0)
    log_gap = jnp.where(pair_mask, cumulative[:, None] - cumulative[None, :], 0.0)
    decay_mat = jnp.where(pair_mask, jnp.exp(log_gap), 0.0)
    gram_mat = jnp.dot(c_block.T, b_block, precision=HIGH)
    scaled_in = x_block * dt_block[None, :]
    y_inner = jnp.dot(scaled_in, (gram_mat * decay_mat).T, precision=HIGH)
    decay_in = jnp.where(seg_block == prev_seg, jnp.exp(cumulative), 0.0)
    y_block = y_inner + jnp.dot(state_in, c_block, precision=HIGH) * decay_in[None, :] + skip_gain * x_block
    last_seg = seg_block[-1]
    weight_out = jnp.where(seg_block == last_seg, jnp.exp(cumulative[-1] - cumulative), 0.0)
    decay_all = jnp.where(last_seg == prev_seg, jnp.exp(cumulative[-1]), 0.0)
    state_out = decay_all * state_in + jnp.dot(scaled_in * weight_out[None, :], b_block.T, precision=HIGH)
    return (state_out, y_block)

def run_head(x_head, dt_head, b_vals, c_vals, segment, before_first, decay_rate, skip_gain, start_state, block_len):
    width_p = x_head.shape[0]
    width_n = b_vals.shape[0]
    block_count = x_head.shape[1] // block_len
    x_blocks = x_head.reshape(width_p, block_count, block_len).transpose(1, 0, 2)
    dt_blocks = dt_head.reshape(block_count, block_len)
    b_blocks = b_vals.reshape(width_n, block_count, block_len).transpose(1, 0, 2)
    c_blocks = c_vals.reshape(width_n, block_count, block_len).transpose(1, 0, 2)
    seg_blocks = segment.reshape(block_count, block_len)
    shifted = jnp.concatenate([before_first.reshape(1).astype(jnp.int32), segment[:-1].astype(jnp.int32)])
    prev_segs = shifted.reshape(block_count, block_len)[:, 0]
    lower_ones = (lax.broadcasted_iota(jnp.int32, (block_len, block_len), 0) >= lax.broadcasted_iota(jnp.int32, (block_len, block_len), 1)).astype(jnp.float32)

    def advance(carry_state, block_data):
        return mixing_block(carry_state, block_data, decay_rate, skip_gain, lower_ones)
    end_state, y_blocks = lax.scan(advance, start_state, (x_blocks, dt_blocks, b_blocks, c_blocks, seg_blocks, prev_segs))
    return (y_blocks.transpose(1, 0, 2).reshape(width_p, -1), end_state)

def reference(inputs, dt, decay_rate, skip, b_proj, c_proj, lengths, grad_out):
    doc_ends = jnp.cumsum(lengths).astype(jnp.int32)
    positions = jnp.arange(SEQ, dtype=jnp.int32)
    segment = lax.optimization_barrier(jnp.sum((positions[None, :] >= doc_ends[:-1, None]).astype(jnp.int32), axis=0)).astype(jnp.int32)
    before_first = jnp.full((), -1, jnp.int32)
    b_float = b_proj.astype(jnp.float32)
    c_float = c_proj.astype(jnp.float32)
    zero_state = jnp.zeros((P_SIZE, N), jnp.float32)

    def one_head(totals, head_data):
        x_head, dt_head, rate_head, skip_head, grad_head = head_data

        def forward(x_vals, dt_vals, b_vals, c_vals):
            return run_head(x_vals, dt_vals, b_vals, c_vals, segment, before_first, rate_head, skip_head, zero_state, BLOCK)[0]
        y_head, pull_back = jax.vjp(forward, x_head.astype(jnp.float32), dt_head, b_float, c_float)
        grad_x, grad_step, grad_bv, grad_cv = pull_back(grad_head.astype(jnp.float32))
        return ((totals[0] + grad_bv, totals[1] + grad_cv), (y_head.astype(jnp.bfloat16), grad_x.astype(jnp.bfloat16), grad_step))
    start_totals = (jnp.zeros((N, SEQ), jnp.float32), jnp.zeros((N, SEQ), jnp.float32))
    (grad_b, grad_c), (mixed, grad_inputs, grad_dt) = lax.scan(one_head, start_totals, (inputs, dt, decay_rate, skip, grad_out))
    return (mixed, grad_inputs, grad_dt, grad_b, grad_c)
```

```python
import functools
import jax
import jax.numpy as jnp
from jax import lax
from jax.experimental import pallas as pl
from jax.experimental.pallas import tpu as pltpu
from jax.sharding import PartitionSpec as P

Q = 128
HIGH = lax.Precision.HIGHEST
F32 = jnp.float32
BF16 = jnp.bfloat16
MESH = pl.DeviceIdType.MESH


def mm(a, b, ca, cb):
    return lax.dot_general(a, b, (((ca,), (cb,)), ((), ())), preferred_element_type=F32)


def split(v):
    hi = v.astype(BF16)
    return hi, (v - hi.astype(F32)).astype(BF16)


def lanes(a, b):
    return jnp.concatenate([a, b], axis=1)


def rows(a, b):
    return jnp.concatenate([a, b], axis=0)


def kernel(cfg, rate_ref, skip_ref, len_ref, x_ref, dt_ref, b_ref, c_ref, g_ref, *refs):
    n_ctx, n_head, hops, fused, ndoc = cfg
    mixed_ref, gx_ref, gdt_ref, gb_ref, gc_ref = refs[:5]
    (s_ref, gz_ref, y_ref, v_ref, out_s, out_g, in_s, in_g, ctx_send, ctx_recv) = refs[5:15]
    if fused:
        part, recv1, send2, recv2, s1_send, s1_recv, s2_send, s2_recv = refs[15:]
    width_p = x_ref.shape[1]
    local = x_ref.shape[2]
    width_n = b_ref.shape[0]
    blocks = local // Q
    me = lax.axis_index("ctx")
    head = lax.axis_index("head")
    chips = n_head // 2
    core = lax.rem(head, 2)
    chip = head // 2

    barrier = pltpu.get_barrier_semaphore()

    @pl.when(me > 0)
    def _():
        pl.semaphore_signal(barrier, inc=1, device_id={"ctx": me - 1}, device_id_type=MESH)

    @pl.when(me < n_ctx - 1)
    def _():
        pl.semaphore_signal(barrier, inc=1, device_id={"ctx": me + 1}, device_id_type=MESH)

    if fused:
        pl.semaphore_signal(
            barrier, inc=1, device_id={"head": chip * 2 + 1 - core}, device_id_type=MESH
        )
        for d in range(1, chips):
            to = lax.rem(chip + d, chips) * 2 + core
            pl.semaphore_signal(barrier, inc=1, device_id={"head": to}, device_id_type=MESH)

    rate = rate_ref[0]
    skip = skip_ref[0]
    offset = me * local

    ends = []
    total = len_ref[0]
    for j in range(ndoc - 1):
        ends.append(total)
        total = total + len_ref[j + 1]

    def segment_of(pos):
        seg = jnp.zeros(pos.shape, jnp.int32)
        for end in ends:
            seg = seg + (pos >= end).astype(jnp.int32)
        return seg

    pos8 = (
        offset
        + lax.broadcasted_iota(jnp.int32, (blocks, Q), 0) * Q
        + lax.broadcasted_iota(jnp.int32, (blocks, Q), 1)
    )
    pos_t = (
        offset
        + lax.broadcasted_iota(jnp.int32, (Q, blocks), 1) * Q
        + lax.broadcasted_iota(jnp.int32, (Q, blocks), 0)
    )
    seg8 = segment_of(pos8)
    seg_t = segment_of(pos_t)
    before8 = jnp.where(pos8 == 0, -1, segment_of(pos8 - 1))
    prev8 = before8[:, 0:1]
    last8 = seg8[:, Q - 1 : Q]

    dt8 = jnp.concatenate([dt_ref[0:1, k * Q : (k + 1) * Q] for k in range(blocks)], axis=0)
    row_i = lax.broadcasted_iota(jnp.int32, (Q, Q), 0)
    col_j = lax.broadcasted_iota(jnp.int32, (Q, Q), 1)
    lower = row_i >= col_j
    lower_ones = lower.astype(F32)
    log8 = -rate * dt8
    cum8 = lax.dot_general(
        log8, lower_ones, (((1,), (1,)), ((), ())), precision=HIGH, preferred_element_type=F32
    )
    cum_t = lax.dot_general(
        lower_ones, log8, (((1,), (1,)), ((), ())), precision=HIGH, preferred_element_type=F32
    )
    end8 = cum8[:, Q - 1 : Q]
    din8 = jnp.where(seg8 == prev8, jnp.exp(cum8), 0.0)
    wdt8 = jnp.where(seg8 == last8, jnp.exp(end8 - cum8), 0.0) * dt8
    dall8 = jnp.where(last8 == prev8, jnp.exp(end8), 0.0)

    def cut(ref, k):
        return ref[0, :, k * Q : (k + 1) * Q]

    def cut2(ref, k):
        return ref[:, k * Q : (k + 1) * Q]

    state = jnp.zeros((width_p, width_n), F32)
    for k in range(blocks):
        s_ref[k] = state
        b_k = cut2(b_ref, k)
        hi, lo = split(cut(x_ref, k).astype(F32) * wdt8[k : k + 1])
        state = dall8[k : k + 1] * state + mm(lanes(hi, lo), lanes(b_k, b_k), 1, 1)
    out_s[0] = state
    carry = jnp.zeros((width_p, width_n), F32)
    for k in reversed(range(blocks)):
        gz_ref[k] = carry
        c_k = cut2(c_ref, k)
        hi, lo = split(cut(g_ref, k).astype(F32) * din8[k : k + 1])
        carry = dall8[k : k + 1] * carry + mm(lanes(hi, lo), lanes(c_k, c_k), 1, 1)
    out_g[0] = carry

    ahead = [None] * blocks
    prod = jnp.ones((1, 1), F32)
    for k in range(blocks):
        ahead[k] = prod
        prod = prod * dall8[k : k + 1]
    decay_dev = prod
    behind = [None] * blocks
    prod = jnp.ones((1, 1), F32)
    for k in reversed(range(blocks)):
        behind[k] = prod
        prod = prod * dall8[k : k + 1]

    @pl.when(me == 0)
    def _():
        in_s[...] = jnp.zeros_like(in_s)

    @pl.when(me == n_ctx - 1)
    def _():
        in_g[...] = jnp.zeros_like(in_g)

    peers = chips if fused else 0
    at_end = (me == 0) | (me == n_ctx - 1)

    @pl.when(at_end)
    def _():
        pl.semaphore_wait(barrier, peers + 1)

    @pl.when(jnp.logical_not(at_end))
    def _():
        pl.semaphore_wait(barrier, peers + 2)

    def ctx_copy(r, way):
        src, dst = (out_s, in_s) if way == 0 else (out_g, in_g)
        return pltpu.make_async_remote_copy(
            src_ref=src.at[r],
            dst_ref=dst.at[r],
            send_sem=ctx_send.at[r, way],
            recv_sem=ctx_recv.at[r, way],
            device_id={"ctx": me + 1 if way == 0 else me - 1},
            device_id_type=MESH,
        )

    def ctx_start(r):
        @pl.when(me < n_ctx - 1)
        def _():
            ctx_copy(r, 0).start()

        @pl.when(me > 0)
        def _():
            ctx_copy(r, 1).start()

    def ctx_wait(r):
        @pl.when(me > 0)
        def _():
            ctx_copy(r, 0).wait_recv()

        @pl.when(me < n_ctx - 1)
        def _():
            ctx_copy(r, 1).wait_recv()

    def ctx_done(r):
        @pl.when(me < n_ctx - 1)
        def _():
            ctx_copy(r, 0).wait_send()

        @pl.when(me > 0)
        def _():
            ctx_copy(r, 1).wait_send()

    ctx_start(0)

    def put(k, way, value, add):
        if fused:
            each = width_n // n_head
            chunk, lo = k // 2, (k % 2) * Q
            for h in range(n_head):
                at = (chunk, h % 2, h // 2, slice(way * each, (way + 1) * each), slice(lo, lo + Q))
                piece = value[h * each : (h + 1) * each]
                part[at] = part[at] + piece if add else piece
        else:
            ref = (gb_ref, gc_ref)[way]
            at = (slice(None), slice(k * Q, (k + 1) * Q))
            ref[at] = ref[at] + value if add else value

    def intra(k):
        x_k, g_k, b_k, c_k = cut(x_ref, k), cut(g_ref, k), cut2(b_ref, k), cut2(c_ref, k)
        mask = lower & (seg_t[:, k : k + 1] == seg8[k : k + 1])
        gap = jnp.where(mask, cum_t[:, k : k + 1] - cum8[k : k + 1], 0.0)
        ddt = jnp.where(mask, jnp.exp(gap), 0.0) * dt8[k : k + 1]
        a_hi, a_lo = split(mm(c_k, b_k, 0, 0) * ddt)
        w_hi, w_lo = split(mm(g_k, x_k, 0, 0) * ddt)
        y_ref[:, k * Q : (k + 1) * Q] = mm(lanes(x_k, x_k), lanes(a_hi, a_lo), 1, 1)
        v_ref[:, k * Q : (k + 1) * Q] = mm(lanes(g_k, g_k), rows(a_hi, a_lo), 1, 0)
        put(k, 0, mm(lanes(c_k, c_k), rows(w_hi, w_lo), 1, 0), False)
        put(k, 1, mm(lanes(b_k, b_k), lanes(w_hi, w_lo), 1, 1), False)

    diffs, qs, tails = [None] * blocks, [None] * blocks, [None] * blocks

    def start_state(k, state_in):
        return s_ref[k] + ahead[k] * state_in

    def inter(k, state_in, grad_in):
        x_k, g_k, b_k, c_k = cut(x_ref, k), cut(g_ref, k), cut2(b_ref, k), cut2(c_ref, k)
        s_k = start_state(k, state_in)
        gz = gz_ref[k] + behind[k] * grad_in
        if k + 1 < blocks:
            s_end = start_state(k + 1, state_in)
        else:
            s_end = out_s[0] + decay_dev * state_in
        tails[k] = jnp.sum(jnp.sum(gz * s_end, axis=0, keepdims=True), axis=1, keepdims=True)
        s_hi, s_lo = split(s_k)
        z_hi, z_lo = split(gz)
        din, wdt = din8[k : k + 1], wdt8[k : k + 1]
        at = (slice(None), slice(k * Q, (k + 1) * Q))
        y = y_ref[at] + mm(lanes(s_hi, s_lo), rows(c_k, c_k), 1, 0) * din
        v = v_ref[at] + mm(lanes(z_hi, z_lo), rows(b_k, b_k), 1, 0) * wdt
        x_f, g_f = x_k.astype(F32), g_k.astype(F32)
        mixed_ref[0, :, k * Q : (k + 1) * Q] = (y + skip * x_f).astype(BF16)
        gx_ref[0, :, k * Q : (k + 1) * Q] = (v + skip * g_f).astype(BF16)
        q_k = jnp.sum(x_f * v, axis=0, keepdims=True)
        qs[k] = q_k
        diffs[k] = jnp.sum(g_f * y, axis=0, keepdims=True) - q_k
        put(k, 0, mm(rows(z_hi, z_lo), rows(x_k, x_k), 0, 0) * wdt, True)
        put(k, 1, mm(rows(s_hi, s_lo), rows(g_k, g_k), 0, 0) * din, True)

    def pair_copy(chunk):
        return pltpu.make_async_remote_copy(
            src_ref=part.at[chunk, 1 - core],
            dst_ref=recv1.at[chunk],
            send_sem=s1_send.at[chunk],
            recv_sem=s1_recv.at[chunk],
            device_id={"head": chip * 2 + 1 - core},
            device_id_type=MESH,
        )

    def chip_copy(chunk, d):
        to = lax.rem(chip + d, chips)
        return pltpu.make_async_remote_copy(
            src_ref=send2.at[chunk, to],
            dst_ref=recv2.at[chunk, d - 1],
            send_sem=s2_send.at[chunk, d - 1],
            recv_sem=s2_recv.at[chunk, d - 1],
            device_id={"head": to * 2 + core},
            device_id_type=MESH,
        )

    def second(chunk):
        pair_copy(chunk).wait_recv()
        send2[chunk] = part[chunk, core] + recv1[chunk]
        for d in range(1, chips):
            chip_copy(chunk, d).start()

    early = blocks // 2
    for k in range(early):
        intra(k)
    ctx_wait(0)
    for r in range(1, hops):
        out_s[r] = out_s[0] + decay_dev * in_s[r - 1]
        out_g[r] = out_g[0] + decay_dev * in_g[r - 1]
        ctx_start(r)
        ctx_wait(r)
    state_in = in_s[hops - 1]
    grad_in = in_g[hops - 1]
    for k in range(blocks):
        if k >= early:
            intra(k)
        inter(k, state_in, grad_in)
        if fused and k % 2 == 1:
            chunk = k // 2
            pair_copy(chunk).start()
            if chunk > 0:
                second(chunk - 1)

    q8 = jnp.concatenate(qs, axis=0)
    r8 = jnp.concatenate(diffs, axis=0)
    tail8 = jnp.concatenate(tails, axis=0)
    back8 = lax.dot_general(
        r8, lower_ones, (((1,), (0,)), ((), ())), precision=HIGH, preferred_element_type=F32
    )
    gdt8 = q8 / dt8 - rate * (back8 + tail8)
    for k in range(blocks):
        gdt_ref[0:1, k * Q : (k + 1) * Q] = gdt8[k : k + 1]

    for r in range(hops):
        ctx_done(r)
    if fused:
        each = width_n // n_head
        chunks = blocks // 2
        second(chunks - 1)
        for chunk in range(chunks):
            total = send2[chunk, chip]
            for d in range(1, chips):
                chip_copy(chunk, d).wait_recv()
                total = total + recv2[chunk, d - 1]
            at = slice(chunk * 2 * Q, (chunk + 1) * 2 * Q)
            gb_ref[:, at] = total[:each]
            gc_ref[:, at] = total[each:]
        for chunk in range(chunks):
            pair_copy(chunk).wait_send()
            for d in range(1, chips):
                chip_copy(chunk, d).wait_send()


def per_device(n_ctx, n_head, inputs, dt, decay_rate, skip, b_proj, c_proj, lengths, grad_out):
    _, width_p, local = inputs.shape
    width_n = b_proj.shape[0]
    longest = n_ctx * local // 4
    hops = max(1, min(n_ctx - 1, (longest - 2) // local + 1))
    each = width_n // n_head
    fused = each % 8 == 0
    blocks = local // Q
    chips = n_head // 2
    chunks = blocks // 2
    vmem = pl.BlockSpec(memory_space=pltpu.VMEM)
    smem = pl.BlockSpec(memory_space=pltpu.SMEM)
    grad_rows = each if fused else width_n
    scratch = [
        pltpu.VMEM((blocks, width_p, width_n), F32),
        pltpu.VMEM((blocks, width_p, width_n), F32),
        pltpu.VMEM((width_p, local), F32),
        pltpu.VMEM((width_p, local), F32),
        pltpu.VMEM((hops, width_p, width_n), F32),
        pltpu.VMEM((hops, width_p, width_n), F32),
        pltpu.VMEM((hops, width_p, width_n), F32),
        pltpu.VMEM((hops, width_p, width_n), F32),
        pltpu.SemaphoreType.DMA((hops, 2)),
        pltpu.SemaphoreType.DMA((hops, 2)),
    ]
    if fused:
        scratch += [
            pltpu.VMEM((chunks, 2, chips, 2 * each, 2 * Q), F32),
            pltpu.VMEM((chunks, chips, 2 * each, 2 * Q), F32),
            pltpu.VMEM((chunks, chips, 2 * each, 2 * Q), F32),
            pltpu.VMEM((chunks, chips - 1, 2 * each, 2 * Q), F32),
            pltpu.SemaphoreType.DMA((chunks,)),
            pltpu.SemaphoreType.DMA((chunks,)),
            pltpu.SemaphoreType.DMA((chunks, chips - 1)),
            pltpu.SemaphoreType.DMA((chunks, chips - 1)),
        ]
    mixed, gx, gdt, gb, gc = pl.pallas_call(
        functools.partial(kernel, (n_ctx, n_head, hops, fused, lengths.shape[0])),
        out_shape=(
            jax.ShapeDtypeStruct(inputs.shape, BF16),
            jax.ShapeDtypeStruct(inputs.shape, BF16),
            jax.ShapeDtypeStruct(dt.shape, F32),
            jax.ShapeDtypeStruct((grad_rows, local), F32),
            jax.ShapeDtypeStruct((grad_rows, local), F32),
        ),
        in_specs=[smem, smem, smem, vmem, vmem, vmem, vmem, vmem],
        out_specs=(vmem,) * 5,
        scratch_shapes=scratch,
        compiler_params=pltpu.CompilerParams(collective_id=0, has_side_effects=True),
    )(decay_rate, skip, lengths, inputs, dt, b_proj, c_proj, grad_out)
    if not fused:
        gb = lax.psum_scatter(gb, "head", scatter_dimension=0, tiled=True)
        gc = lax.psum_scatter(gc, "head", scatter_dimension=0, tiled=True)
    return mixed, gx, gdt, gb, gc


def solution(mesh):
    return jax.shard_map(
        functools.partial(per_device, mesh.shape["ctx"], mesh.shape["head"]),
        mesh=mesh,
        in_specs=(
            P("head", None, "ctx"),
            P("head", "ctx"),
            P("head"),
            P("head"),
            P(None, "ctx"),
            P(None, "ctx"),
            P(),
            P("head", None, "ctx"),
        ),
        out_specs=(
            P("head", None, "ctx"),
            P("head", None, "ctx"),
            P("head", "ctx"),
            P("head", "ctx"),
            P("head", "ctx"),
        ),
        check_vma=False,
    )
```

```python
import functools
import jax
import jax.numpy as jnp
from jax import lax
from jax.experimental import pallas as pl
from jax.experimental.pallas import tpu as pltpu
from jax.sharding import PartitionSpec as P

Q = 128
SCHEDULE = ((0, 2), (1, 3, 5, 6))
HIGH = lax.Precision.HIGHEST
F32 = jnp.float32
BF16 = jnp.bfloat16
MESH = pl.DeviceIdType.MESH


def mm(a, b, ca, cb):
    return lax.dot_general(a, b, (((ca,), (cb,)), ((), ())), preferred_element_type=F32)


def split(v):
    hi = v.astype(BF16)
    return hi, (v - hi.astype(F32)).astype(BF16)


def lanes(a, b):
    return jnp.concatenate([a, b], axis=1)


def rows(a, b):
    return jnp.concatenate([a, b], axis=0)


def kernel(cfg, rate_ref, skip_ref, len_ref, x_ref, dt_ref, b_ref, c_ref, g_ref, *refs):
    n_ctx, n_head, hops, fused, ndoc = cfg
    mixed_ref, gx_ref, gdt_ref, gb_ref, gc_ref = refs[:5]
    (s_ref, gz_ref, ddt_ref, out_s, out_g, in_s, in_g, ctx_send, ctx_recv) = refs[5:14]
    if fused:
        part, recv1, summed, recv2, later, recv3, sems_send, sems_recv = refs[14:]
    width_p = x_ref.shape[1]
    local = x_ref.shape[2]
    width_n = b_ref.shape[0]
    blocks = local // Q
    me = lax.axis_index("ctx")
    head = lax.axis_index("head")
    core = lax.rem(head, 2)
    at_x = lax.rem(head // 2, 2)
    at_y = head // 4
    pair_peer = head + 1 - 2 * core
    x_peer = head + 2 - 4 * at_x
    y_peer = head + 4 - 8 * at_y

    barrier = pltpu.get_barrier_semaphore()

    @pl.when(me > 0)
    def _():
        pl.semaphore_signal(barrier, inc=1, device_id={"ctx": me - 1}, device_id_type=MESH)

    @pl.when(me < n_ctx - 1)
    def _():
        pl.semaphore_signal(barrier, inc=1, device_id={"ctx": me + 1}, device_id_type=MESH)

    if fused:
        for peer in (pair_peer, x_peer, y_peer):
            pl.semaphore_signal(barrier, inc=1, device_id={"head": peer}, device_id_type=MESH)

    rate = rate_ref[0]
    skip = skip_ref[0]
    offset = me * local

    ends = []
    total = len_ref[0]
    for j in range(ndoc - 1):
        ends.append(total)
        total = total + len_ref[j + 1]

    def segment_of(pos):
        seg = jnp.zeros(pos.shape, jnp.int32)
        for end in ends:
            seg = seg + (pos >= end).astype(jnp.int32)
        return seg

    pos8 = (
        offset
        + lax.broadcasted_iota(jnp.int32, (blocks, Q), 0) * Q
        + lax.broadcasted_iota(jnp.int32, (blocks, Q), 1)
    )
    pos_t = (
        offset
        + lax.broadcasted_iota(jnp.int32, (Q, blocks), 1) * Q
        + lax.broadcasted_iota(jnp.int32, (Q, blocks), 0)
    )
    seg8 = segment_of(pos8)
    seg_t = segment_of(pos_t)
    before8 = jnp.where(pos8 == 0, -1, segment_of(pos8 - 1))
    prev8 = before8[:, 0:1]
    last8 = seg8[:, Q - 1 : Q]

    dt8 = jnp.concatenate([dt_ref[0:1, k * Q : (k + 1) * Q] for k in range(blocks)], axis=0)
    row_i = lax.broadcasted_iota(jnp.int32, (Q, Q), 0)
    col_j = lax.broadcasted_iota(jnp.int32, (Q, Q), 1)
    lower = row_i >= col_j
    lower_ones = lower.astype(F32)
    log8 = -rate * dt8
    cum8 = lax.dot_general(
        log8, lower_ones, (((1,), (1,)), ((), ())), precision=HIGH, preferred_element_type=F32
    )
    cum_t = lax.dot_general(
        lower_ones, log8, (((1,), (1,)), ((), ())), precision=HIGH, preferred_element_type=F32
    )
    end8 = cum8[:, Q - 1 : Q]
    din8 = jnp.where(seg8 == prev8, jnp.exp(cum8), 0.0)
    wdt8 = jnp.where(seg8 == last8, jnp.exp(end8 - cum8), 0.0) * dt8
    dall8 = jnp.where(last8 == prev8, jnp.exp(end8), 0.0)

    def cut(ref, k):
        return ref[0, :, k * Q : (k + 1) * Q]

    def cut2(ref, k):
        return ref[:, k * Q : (k + 1) * Q]

    state = jnp.zeros((width_p, width_n), F32)
    for k in range(blocks):
        s_ref[k] = state
        b_k = cut2(b_ref, k)
        hi, lo = split(cut(x_ref, k).astype(F32) * wdt8[k : k + 1])
        state = dall8[k : k + 1] * state + mm(lanes(hi, lo), lanes(b_k, b_k), 1, 1)
    out_s[0] = state

    def ctx_copy(r, way):
        src, dst = (out_s, in_s) if way == 0 else (out_g, in_g)
        return pltpu.make_async_remote_copy(
            src_ref=src.at[r],
            dst_ref=dst.at[r],
            send_sem=ctx_send.at[r, way],
            recv_sem=ctx_recv.at[r, way],
            device_id={"ctx": me + 1 if way == 0 else me - 1},
            device_id_type=MESH,
        )

    def ctx_start_s(r):
        @pl.when(me < n_ctx - 1)
        def _():
            ctx_copy(r, 0).start()

    def ctx_start_g(r):
        @pl.when(me > 0)
        def _():
            ctx_copy(r, 1).start()

    def ctx_wait(r):
        @pl.when(me > 0)
        def _():
            ctx_copy(r, 0).wait_recv()

        @pl.when(me < n_ctx - 1)
        def _():
            ctx_copy(r, 1).wait_recv()

    def ctx_done(r):
        @pl.when(me < n_ctx - 1)
        def _():
            ctx_copy(r, 0).wait_send()

        @pl.when(me > 0)
        def _():
            ctx_copy(r, 1).wait_send()

    @pl.when(me == 0)
    def _():
        in_s[...] = jnp.zeros_like(in_s)

    @pl.when(me == n_ctx - 1)
    def _():
        in_g[...] = jnp.zeros_like(in_g)

    peers = 3 if fused else 0
    at_end = (me == 0) | (me == n_ctx - 1)

    @pl.when(at_end)
    def _():
        pl.semaphore_wait(barrier, peers + 1)

    @pl.when(jnp.logical_not(at_end))
    def _():
        pl.semaphore_wait(barrier, peers + 2)

    ctx_start_s(0)
    carry = jnp.zeros((width_p, width_n), F32)
    for k in reversed(range(blocks)):
        gz_ref[k] = carry
        c_k = cut2(c_ref, k)
        hi, lo = split(cut(g_ref, k).astype(F32) * din8[k : k + 1])
        carry = dall8[k : k + 1] * carry + mm(lanes(hi, lo), lanes(c_k, c_k), 1, 1)
    out_g[0] = carry
    ctx_start_g(0)

    ahead = [None] * blocks
    prod = jnp.ones((1, 1), F32)
    for k in range(blocks):
        ahead[k] = prod
        prod = prod * dall8[k : k + 1]
    decay_dev = prod
    behind = [None] * blocks
    prod = jnp.ones((1, 1), F32)
    for k in reversed(range(blocks)):
        behind[k] = prod
        prod = prod * dall8[k : k + 1]

    def put(k, way, value, add):
        if fused:
            each = width_n // n_head
            chunk, lo = k // 2, (k % 2) * Q
            for h in range(n_head):
                c, x, y = h % 2, (h // 2) % 2, h // 4
                one, two = (x, y) if way == 0 else (y, x)
                at = (chunk, c, way, one, two, slice(None), slice(lo, lo + Q))
                piece = value[h * each : (h + 1) * each]
                part[at] = part[at] + piece if add else piece
        else:
            ref = (gb_ref, gc_ref)[way]
            at = (slice(None), slice(k * Q, (k + 1) * Q))
            ref[at] = ref[at] + value if add else value

    def intra_w(k):
        x_k, g_k, b_k, c_k = cut(x_ref, k), cut(g_ref, k), cut2(b_ref, k), cut2(c_ref, k)
        mask = lower & (seg_t[:, k : k + 1] == seg8[k : k + 1])
        gap = jnp.where(mask, cum_t[:, k : k + 1] - cum8[k : k + 1], 0.0)
        ddt = jnp.where(mask, jnp.exp(gap), 0.0) * dt8[k : k + 1]
        ddt_ref[k] = ddt
        w_hi, w_lo = split(mm(g_k, x_k, 0, 0) * ddt)
        put(k, 0, mm(lanes(c_k, c_k), rows(w_hi, w_lo), 1, 0), False)
        put(k, 1, mm(lanes(b_k, b_k), lanes(w_hi, w_lo), 1, 1), False)

    diffs, qs, tails = [None] * blocks, [None] * blocks, [None] * blocks

    def inter_w(k, state_in, grad_in):
        x_k, g_k = cut(x_ref, k), cut(g_ref, k)
        s_k = s_ref[k] + ahead[k] * state_in
        gz = gz_ref[k] + behind[k] * grad_in
        s_ref[k] = s_k
        gz_ref[k] = gz
        s_hi, s_lo = split(s_k)
        z_hi, z_lo = split(gz)
        put(k, 0, mm(rows(z_hi, z_lo), rows(x_k, x_k), 0, 0) * wdt8[k : k + 1], True)
        put(k, 1, mm(rows(s_hi, s_lo), rows(g_k, g_k), 0, 0) * din8[k : k + 1], True)

    def outer(k, state_in):
        x_k, g_k, b_k, c_k = cut(x_ref, k), cut(g_ref, k), cut2(b_ref, k), cut2(c_ref, k)
        s_k = s_ref[k]
        gz = gz_ref[k]
        s_end = s_ref[k + 1] if k + 1 < blocks else out_s[0] + decay_dev * state_in
        tails[k] = jnp.sum(jnp.sum(gz * s_end, axis=0, keepdims=True), axis=1, keepdims=True)
        a_hi, a_lo = split(mm(c_k, b_k, 0, 0) * ddt_ref[k])
        s_hi, s_lo = split(s_k)
        z_hi, z_lo = split(gz)
        din, wdt = din8[k : k + 1], wdt8[k : k + 1]
        y = mm(lanes(x_k, x_k), lanes(a_hi, a_lo), 1, 1)
        y = y + mm(lanes(s_hi, s_lo), rows(c_k, c_k), 1, 0) * din
        v = mm(lanes(g_k, g_k), rows(a_hi, a_lo), 1, 0)
        v = v + mm(lanes(z_hi, z_lo), rows(b_k, b_k), 1, 0) * wdt
        x_f, g_f = x_k.astype(F32), g_k.astype(F32)
        mixed_ref[0, :, k * Q : (k + 1) * Q] = (y + skip * x_f).astype(BF16)
        gx_ref[0, :, k * Q : (k + 1) * Q] = (v + skip * g_f).astype(BF16)
        q_k = jnp.sum(x_f * v, axis=0, keepdims=True)
        qs[k] = q_k
        diffs[k] = jnp.sum(g_f * y, axis=0, keepdims=True) - q_k

    coord = (at_x, at_y)
    peer_of = (x_peer, y_peer)

    def hop(src, dst, chunk, stage, to):
        return pltpu.make_async_remote_copy(
            src_ref=src,
            dst_ref=dst,
            send_sem=sems_send.at[chunk, stage],
            recv_sem=sems_recv.at[chunk, stage],
            device_id={"head": to},
            device_id_type=MESH,
        )

    def pair_copy(chunk):
        return hop(part.at[chunk, 1 - core], recv1.at[chunk], chunk, 0, pair_peer)

    def first_copy(chunk, way):
        src = summed.at[chunk, way, 1 - coord[way]]
        return hop(src, recv2.at[chunk, way], chunk, 1 + way, peer_of[way])

    def second_copy(chunk, way):
        src = later.at[chunk, way, 1 - coord[1 - way]]
        return hop(src, recv3.at[chunk, way], chunk, 3 + way, peer_of[1 - way])

    def first(chunk):
        pair_copy(chunk).wait_recv()
        summed[chunk] = part[chunk, core] + recv1[chunk]
        for way in range(2):
            first_copy(chunk, way).start()

    def second(chunk):
        for way in range(2):
            first_copy(chunk, way).wait_recv()
            later[chunk, way] = summed[chunk, way, coord[way]] + recv2[chunk, way]
            second_copy(chunk, way).start()

    for k in range(blocks):
        intra_w(k)
    ctx_wait(0)
    for r in range(1, hops):
        out_s[r] = out_s[0] + decay_dev * in_s[r - 1]
        out_g[r] = out_g[0] + decay_dev * in_g[r - 1]
        ctx_start_s(r)
        ctx_start_g(r)
        ctx_wait(r)
    state_in = in_s[hops - 1]
    grad_in = in_g[hops - 1]
    for k in range(blocks):
        inter_w(k, state_in, grad_in)
        if fused and k % 2 == 1:
            pair_copy(k // 2).start()
            if k >= 5:
                first(k // 2 - 2)
    chunks = blocks // 2
    firsts, seconds = SCHEDULE
    for k in range(blocks):
        if fused:
            for chunk in range(chunks):
                if chunk >= chunks - 2 and firsts[chunk - chunks + 2] == k:
                    first(chunk)
                if seconds[chunk] == k:
                    second(chunk)
        outer(k, state_in)

    q8 = jnp.concatenate(qs, axis=0)
    r8 = jnp.concatenate(diffs, axis=0)
    tail8 = jnp.concatenate(tails, axis=0)
    back8 = lax.dot_general(
        r8, lower_ones, (((1,), (0,)), ((), ())), precision=HIGH, preferred_element_type=F32
    )
    gdt8 = q8 / dt8 - rate * (back8 + tail8)
    for k in range(blocks):
        gdt_ref[0:1, k * Q : (k + 1) * Q] = gdt8[k : k + 1]

    for r in range(hops):
        ctx_done(r)
    if fused:
        for chunk in range(chunks):
            at = slice(chunk * 2 * Q, (chunk + 1) * 2 * Q)
            for way in range(2):
                second_copy(chunk, way).wait_recv()
                own = later[chunk, way, coord[1 - way]]
                (gb_ref, gc_ref)[way][:, at] = own + recv3[chunk, way]
        for chunk in range(chunks):
            pair_copy(chunk).wait_send()
            for way in range(2):
                first_copy(chunk, way).wait_send()
                second_copy(chunk, way).wait_send()


def move(*refs):
    count = len(refs) // 2
    for i in range(count):
        refs[count + i][...] = refs[i][...]


def per_device(n_ctx, n_head, inputs, dt, decay_rate, skip, b_proj, c_proj, lengths, grad_out):
    _, width_p, local = inputs.shape
    width_n = b_proj.shape[0]
    longest = n_ctx * local // 4
    hops = max(1, min(n_ctx - 1, (longest - 2) // local + 1))
    each = width_n // n_head
    fused = n_head == 8 and each % 8 == 0 and local == 8 * Q
    blocks = local // Q
    chunks = blocks // 2
    vmem = pl.BlockSpec(memory_space=pltpu.VMEM)
    smem = pl.BlockSpec(memory_space=pltpu.SMEM)
    grad_rows = each if fused else width_n
    scratch = [
        pltpu.VMEM((blocks, width_p, width_n), F32),
        pltpu.VMEM((blocks, width_p, width_n), F32),
        pltpu.VMEM((blocks, Q, Q), F32),
        pltpu.VMEM((hops, width_p, width_n), F32),
        pltpu.VMEM((hops, width_p, width_n), F32),
        pltpu.VMEM((hops, width_p, width_n), F32),
        pltpu.VMEM((hops, width_p, width_n), F32),
        pltpu.SemaphoreType.DMA((hops, 2)),
        pltpu.SemaphoreType.DMA((hops, 2)),
    ]
    if fused:
        scratch += [
            pltpu.VMEM((chunks, 2, 2, 2, 2, each, 2 * Q), F32),
            pltpu.VMEM((chunks, 2, 2, 2, each, 2 * Q), F32),
            pltpu.VMEM((chunks, 2, 2, 2, each, 2 * Q), F32),
            pltpu.VMEM((chunks, 2, 2, each, 2 * Q), F32),
            pltpu.VMEM((chunks, 2, 2, each, 2 * Q), F32),
            pltpu.VMEM((chunks, 2, each, 2 * Q), F32),
            pltpu.SemaphoreType.DMA((chunks, 5)),
            pltpu.SemaphoreType.DMA((chunks, 5)),
        ]
    mixed, gx, gdt, gb, gc = pl.pallas_call(
        functools.partial(kernel, (n_ctx, n_head, hops, fused, lengths.shape[0])),
        out_shape=(
            jax.ShapeDtypeStruct(inputs.shape, BF16),
            jax.ShapeDtypeStruct(inputs.shape, BF16),
            jax.ShapeDtypeStruct(dt.shape, F32),
            jax.ShapeDtypeStruct((grad_rows, local), F32),
            jax.ShapeDtypeStruct((grad_rows, local), F32),
        ),
        in_specs=[smem, smem, smem, vmem, vmem, vmem, vmem, vmem],
        out_specs=(vmem,) * 5,
        scratch_shapes=scratch,
        compiler_params=pltpu.CompilerParams(collective_id=0, has_side_effects=True),
    )(decay_rate, skip, lengths, inputs, dt, b_proj, c_proj, grad_out)
    if not fused:
        gb = lax.psum_scatter(gb, "head", scatter_dimension=0, tiled=True)
        gc = lax.psum_scatter(gc, "head", scatter_dimension=0, tiled=True)
    results = (mixed, gx, gdt, gb, gc)
    hbm = pl.BlockSpec(memory_space=pltpu.VMEM)
    return pl.pallas_call(
        move,
        out_shape=tuple(jax.ShapeDtypeStruct(r.shape, r.dtype) for r in results),
        in_specs=[hbm] * 5,
        out_specs=(hbm,) * 5,
    )(*results)


def solution(mesh):
    return jax.shard_map(
        functools.partial(per_device, mesh.shape["ctx"], mesh.shape["head"]),
        mesh=mesh,
        in_specs=(
            P("head", None, "ctx"),
            P("head", "ctx"),
            P("head"),
            P("head"),
            P(None, "ctx"),
            P(None, "ctx"),
            P(),
            P("head", None, "ctx"),
        ),
        out_specs=(
            P("head", None, "ctx"),
            P("head", None, "ctx"),
            P("head", "ctx"),
            P("head", "ctx"),
            P("head", "ctx"),
        ),
        check_vma=False,
    )
```

```python
import functools
import jax
import jax.numpy as jnp
from jax import lax
from jax.experimental import pallas as pl
from jax.experimental.pallas import tpu as pltpu
from jax.sharding import PartitionSpec as P

Q = 128
HIGH = lax.Precision.HIGHEST
F32 = jnp.float32
BF16 = jnp.bfloat16
MESH = pl.DeviceIdType.MESH


def mm(a, b, ca, cb):
    return lax.dot_general(a, b, (((ca,), (cb,)), ((), ())), preferred_element_type=F32)


def split(v):
    hi = v.astype(BF16)
    return hi, (v - hi.astype(F32)).astype(BF16)


def lanes(a, b):
    return jnp.concatenate([a, b], axis=1)


def rows(a, b):
    return jnp.concatenate([a, b], axis=0)


def kernel(cfg, rate_ref, skip_ref, len_ref, x_ref, dt_ref, b_ref, c_ref, g_ref, *refs):
    n_ctx, n_head, hops, fused, ndoc = cfg
    mixed_ref, gx_ref, gdt_ref, gb_ref, gc_ref = refs[:5]
    (s_ref, gz_ref, ddt_ref, out_s, out_g, in_s, in_g, ctx_send, ctx_recv) = refs[5:14]
    if fused:
        part, recv1, send2, recv2, s1_send, s1_recv, s2_send, s2_recv = refs[14:]
    width_p = x_ref.shape[1]
    local = x_ref.shape[2]
    width_n = b_ref.shape[0]
    blocks = local // Q
    me = lax.axis_index("ctx")
    head = lax.axis_index("head")
    chips = n_head // 2
    core = lax.rem(head, 2)
    chip = head // 2

    barrier = pltpu.get_barrier_semaphore()

    @pl.when(me > 0)
    def _():
        pl.semaphore_signal(barrier, inc=1, device_id={"ctx": me - 1}, device_id_type=MESH)

    @pl.when(me < n_ctx - 1)
    def _():
        pl.semaphore_signal(barrier, inc=1, device_id={"ctx": me + 1}, device_id_type=MESH)

    if fused:
        pl.semaphore_signal(
            barrier, inc=1, device_id={"head": chip * 2 + 1 - core}, device_id_type=MESH
        )
        for d in range(1, chips):
            to = lax.rem(chip + d, chips) * 2 + core
            pl.semaphore_signal(barrier, inc=1, device_id={"head": to}, device_id_type=MESH)

    rate = rate_ref[0]
    skip = skip_ref[0]
    offset = me * local

    ends = []
    total = len_ref[0]
    for j in range(ndoc - 1):
        ends.append(total)
        total = total + len_ref[j + 1]

    def segment_of(pos):
        seg = jnp.zeros(pos.shape, jnp.int32)
        for end in ends:
            seg = seg + (pos >= end).astype(jnp.int32)
        return seg

    pos8 = (
        offset
        + lax.broadcasted_iota(jnp.int32, (blocks, Q), 0) * Q
        + lax.broadcasted_iota(jnp.int32, (blocks, Q), 1)
    )
    pos_t = (
        offset
        + lax.broadcasted_iota(jnp.int32, (Q, blocks), 1) * Q
        + lax.broadcasted_iota(jnp.int32, (Q, blocks), 0)
    )
    seg8 = segment_of(pos8)
    seg_t = segment_of(pos_t)
    before8 = jnp.where(pos8 == 0, -1, segment_of(pos8 - 1))
    prev8 = before8[:, 0:1]
    last8 = seg8[:, Q - 1 : Q]

    dt8 = jnp.concatenate([dt_ref[0:1, k * Q : (k + 1) * Q] for k in range(blocks)], axis=0)
    row_i = lax.broadcasted_iota(jnp.int32, (Q, Q), 0)
    col_j = lax.broadcasted_iota(jnp.int32, (Q, Q), 1)
    lower = row_i >= col_j
    lower_ones = lower.astype(F32)
    log8 = -rate * dt8
    cum8 = lax.dot_general(
        log8, lower_ones, (((1,), (1,)), ((), ())), precision=HIGH, preferred_element_type=F32
    )
    cum_t = lax.dot_general(
        lower_ones, log8, (((1,), (1,)), ((), ())), precision=HIGH, preferred_element_type=F32
    )
    end8 = cum8[:, Q - 1 : Q]
    din8 = jnp.where(seg8 == prev8, jnp.exp(cum8), 0.0)
    wdt8 = jnp.where(seg8 == last8, jnp.exp(end8 - cum8), 0.0) * dt8
    dall8 = jnp.where(last8 == prev8, jnp.exp(end8), 0.0)

    def cut(ref, k):
        return ref[0, :, k * Q : (k + 1) * Q]

    def cut2(ref, k):
        return ref[:, k * Q : (k + 1) * Q]

    state = jnp.zeros((width_p, width_n), F32)
    for k in range(blocks):
        s_ref[k] = state
        b_k = cut2(b_ref, k)
        hi, lo = split(cut(x_ref, k).astype(F32) * wdt8[k : k + 1])
        state = dall8[k : k + 1] * state + mm(lanes(hi, lo), lanes(b_k, b_k), 1, 1)
    out_s[0] = state
    carry = jnp.zeros((width_p, width_n), F32)
    for k in reversed(range(blocks)):
        gz_ref[k] = carry
        c_k = cut2(c_ref, k)
        hi, lo = split(cut(g_ref, k).astype(F32) * din8[k : k + 1])
        carry = dall8[k : k + 1] * carry + mm(lanes(hi, lo), lanes(c_k, c_k), 1, 1)
    out_g[0] = carry

    ahead = [None] * blocks
    prod = jnp.ones((1, 1), F32)
    for k in range(blocks):
        ahead[k] = prod
        prod = prod * dall8[k : k + 1]
    decay_dev = prod
    behind = [None] * blocks
    prod = jnp.ones((1, 1), F32)
    for k in reversed(range(blocks)):
        behind[k] = prod
        prod = prod * dall8[k : k + 1]

    @pl.when(me == 0)
    def _():
        in_s[...] = jnp.zeros_like(in_s)

    @pl.when(me == n_ctx - 1)
    def _():
        in_g[...] = jnp.zeros_like(in_g)

    peers = chips if fused else 0
    at_end = (me == 0) | (me == n_ctx - 1)

    @pl.when(at_end)
    def _():
        pl.semaphore_wait(barrier, peers + 1)

    @pl.when(jnp.logical_not(at_end))
    def _():
        pl.semaphore_wait(barrier, peers + 2)

    def ctx_copy(r, way):
        src, dst = (out_s, in_s) if way == 0 else (out_g, in_g)
        return pltpu.make_async_remote_copy(
            src_ref=src.at[r],
            dst_ref=dst.at[r],
            send_sem=ctx_send.at[r, way],
            recv_sem=ctx_recv.at[r, way],
            device_id={"ctx": me + 1 if way == 0 else me - 1},
            device_id_type=MESH,
        )

    def ctx_start(r):
        @pl.when(me < n_ctx - 1)
        def _():
            ctx_copy(r, 0).start()

        @pl.when(me > 0)
        def _():
            ctx_copy(r, 1).start()

    def ctx_wait(r):
        @pl.when(me > 0)
        def _():
            ctx_copy(r, 0).wait_recv()

        @pl.when(me < n_ctx - 1)
        def _():
            ctx_copy(r, 1).wait_recv()

    def ctx_done(r):
        @pl.when(me < n_ctx - 1)
        def _():
            ctx_copy(r, 0).wait_send()

        @pl.when(me > 0)
        def _():
            ctx_copy(r, 1).wait_send()

    ctx_start(0)

    def put(k, way, value, add):
        if fused:
            each = width_n // n_head
            chunk, lo = k // 2, (k % 2) * Q
            for h in range(n_head):
                at = (chunk, h % 2, h // 2, slice(way * each, (way + 1) * each), slice(lo, lo + Q))
                piece = value[h * each : (h + 1) * each]
                part[at] = part[at] + piece if add else piece
        else:
            ref = (gb_ref, gc_ref)[way]
            at = (slice(None), slice(k * Q, (k + 1) * Q))
            ref[at] = ref[at] + value if add else value

    def intra_w(k):
        x_k, g_k, b_k, c_k = cut(x_ref, k), cut(g_ref, k), cut2(b_ref, k), cut2(c_ref, k)
        mask = lower & (seg_t[:, k : k + 1] == seg8[k : k + 1])
        gap = jnp.where(mask, cum_t[:, k : k + 1] - cum8[k : k + 1], 0.0)
        ddt = jnp.where(mask, jnp.exp(gap), 0.0) * dt8[k : k + 1]
        ddt_ref[k] = ddt
        w_hi, w_lo = split(mm(g_k, x_k, 0, 0) * ddt)
        put(k, 0, mm(lanes(c_k, c_k), rows(w_hi, w_lo), 1, 0), False)
        put(k, 1, mm(lanes(b_k, b_k), lanes(w_hi, w_lo), 1, 1), False)

    diffs, qs, tails = [None] * blocks, [None] * blocks, [None] * blocks

    def inter_w(k, state_in, grad_in):
        x_k, g_k = cut(x_ref, k), cut(g_ref, k)
        s_k = s_ref[k] + ahead[k] * state_in
        gz = gz_ref[k] + behind[k] * grad_in
        s_ref[k] = s_k
        gz_ref[k] = gz
        s_hi, s_lo = split(s_k)
        z_hi, z_lo = split(gz)
        put(k, 0, mm(rows(z_hi, z_lo), rows(x_k, x_k), 0, 0) * wdt8[k : k + 1], True)
        put(k, 1, mm(rows(s_hi, s_lo), rows(g_k, g_k), 0, 0) * din8[k : k + 1], True)

    def outer(k, state_in):
        x_k, g_k, b_k, c_k = cut(x_ref, k), cut(g_ref, k), cut2(b_ref, k), cut2(c_ref, k)
        s_k = s_ref[k]
        gz = gz_ref[k]
        s_end = s_ref[k + 1] if k + 1 < blocks else out_s[0] + decay_dev * state_in
        tails[k] = jnp.sum(jnp.sum(gz * s_end, axis=0, keepdims=True), axis=1, keepdims=True)
        a_hi, a_lo = split(mm(c_k, b_k, 0, 0) * ddt_ref[k])
        s_hi, s_lo = split(s_k)
        z_hi, z_lo = split(gz)
        din, wdt = din8[k : k + 1], wdt8[k : k + 1]
        y = mm(lanes(x_k, x_k), lanes(a_hi, a_lo), 1, 1)
        y = y + mm(lanes(s_hi, s_lo), rows(c_k, c_k), 1, 0) * din
        v = mm(lanes(g_k, g_k), rows(a_hi, a_lo), 1, 0)
        v = v + mm(lanes(z_hi, z_lo), rows(b_k, b_k), 1, 0) * wdt
        x_f, g_f = x_k.astype(F32), g_k.astype(F32)
        mixed_ref[0, :, k * Q : (k + 1) * Q] = (y + skip * x_f).astype(BF16)
        gx_ref[0, :, k * Q : (k + 1) * Q] = (v + skip * g_f).astype(BF16)
        q_k = jnp.sum(x_f * v, axis=0, keepdims=True)
        qs[k] = q_k
        diffs[k] = jnp.sum(g_f * y, axis=0, keepdims=True) - q_k

    def pair_copy(chunk):
        return pltpu.make_async_remote_copy(
            src_ref=part.at[chunk, 1 - core],
            dst_ref=recv1.at[chunk],
            send_sem=s1_send.at[chunk],
            recv_sem=s1_recv.at[chunk],
            device_id={"head": chip * 2 + 1 - core},
            device_id_type=MESH,
        )

    def chip_copy(chunk, d):
        to = lax.rem(chip + d, chips)
        return pltpu.make_async_remote_copy(
            src_ref=send2.at[chunk, to],
            dst_ref=recv2.at[chunk, d - 1],
            send_sem=s2_send.at[chunk, d - 1],
            recv_sem=s2_recv.at[chunk, d - 1],
            device_id={"head": to * 2 + core},
            device_id_type=MESH,
        )

    def second(chunk):
        pair_copy(chunk).wait_recv()
        send2[chunk] = part[chunk, core] + recv1[chunk]
        for d in range(1, chips):
            chip_copy(chunk, d).start()

    for k in range(blocks):
        intra_w(k)
    ctx_wait(0)
    for r in range(1, hops):
        out_s[r] = out_s[0] + decay_dev * in_s[r - 1]
        out_g[r] = out_g[0] + decay_dev * in_g[r - 1]
        ctx_start(r)
        ctx_wait(r)
    state_in = in_s[hops - 1]
    grad_in = in_g[hops - 1]
    for k in range(blocks):
        inter_w(k, state_in, grad_in)
        if fused and k % 2 == 1:
            pair_copy(k // 2).start()
    for k in range(blocks):
        if fused and k < blocks // 2:
            second(k)
        outer(k, state_in)

    q8 = jnp.concatenate(qs, axis=0)
    r8 = jnp.concatenate(diffs, axis=0)
    tail8 = jnp.concatenate(tails, axis=0)
    back8 = lax.dot_general(
        r8, lower_ones, (((1,), (0,)), ((), ())), precision=HIGH, preferred_element_type=F32
    )
    gdt8 = q8 / dt8 - rate * (back8 + tail8)
    for k in range(blocks):
        gdt_ref[0:1, k * Q : (k + 1) * Q] = gdt8[k : k + 1]

    for r in range(hops):
        ctx_done(r)
    if fused:
        each = width_n // n_head
        chunks = blocks // 2
        for chunk in range(chunks):
            total = send2[chunk, chip]
            for d in range(1, chips):
                chip_copy(chunk, d).wait_recv()
                total = total + recv2[chunk, d - 1]
            at = slice(chunk * 2 * Q, (chunk + 1) * 2 * Q)
            gb_ref[:, at] = total[:each]
            gc_ref[:, at] = total[each:]
        for chunk in range(chunks):
            pair_copy(chunk).wait_send()
            for d in range(1, chips):
                chip_copy(chunk, d).wait_send()


def move(*refs):
    count = len(refs) // 2
    for i in range(count):
        refs[count + i][...] = refs[i][...]


def per_device(n_ctx, n_head, inputs, dt, decay_rate, skip, b_proj, c_proj, lengths, grad_out):
    _, width_p, local = inputs.shape
    width_n = b_proj.shape[0]
    longest = n_ctx * local // 4
    hops = max(1, min(n_ctx - 1, (longest - 2) // local + 1))
    each = width_n // n_head
    fused = each % 8 == 0
    blocks = local // Q
    chips = n_head // 2
    chunks = blocks // 2
    vmem = pl.BlockSpec(memory_space=pltpu.VMEM)
    smem = pl.BlockSpec(memory_space=pltpu.SMEM)
    grad_rows = each if fused else width_n
    scratch = [
        pltpu.VMEM((blocks, width_p, width_n), F32),
        pltpu.VMEM((blocks, width_p, width_n), F32),
        pltpu.VMEM((blocks, Q, Q), F32),
        pltpu.VMEM((hops, width_p, width_n), F32),
        pltpu.VMEM((hops, width_p, width_n), F32),
        pltpu.VMEM((hops, width_p, width_n), F32),
        pltpu.VMEM((hops, width_p, width_n), F32),
        pltpu.SemaphoreType.DMA((hops, 2)),
        pltpu.SemaphoreType.DMA((hops, 2)),
    ]
    if fused:
        scratch += [
            pltpu.VMEM((chunks, 2, chips, 2 * each, 2 * Q), F32),
            pltpu.VMEM((chunks, chips, 2 * each, 2 * Q), F32),
            pltpu.VMEM((chunks, chips, 2 * each, 2 * Q), F32),
            pltpu.VMEM((chunks, chips - 1, 2 * each, 2 * Q), F32),
            pltpu.SemaphoreType.DMA((chunks,)),
            pltpu.SemaphoreType.DMA((chunks,)),
            pltpu.SemaphoreType.DMA((chunks, chips - 1)),
            pltpu.SemaphoreType.DMA((chunks, chips - 1)),
        ]
    mixed, gx, gdt, gb, gc = pl.pallas_call(
        functools.partial(kernel, (n_ctx, n_head, hops, fused, lengths.shape[0])),
        out_shape=(
            jax.ShapeDtypeStruct(inputs.shape, BF16),
            jax.ShapeDtypeStruct(inputs.shape, BF16),
            jax.ShapeDtypeStruct(dt.shape, F32),
            jax.ShapeDtypeStruct((grad_rows, local), F32),
            jax.ShapeDtypeStruct((grad_rows, local), F32),
        ),
        in_specs=[smem, smem, smem, vmem, vmem, vmem, vmem, vmem],
        out_specs=(vmem,) * 5,
        scratch_shapes=scratch,
        compiler_params=pltpu.CompilerParams(collective_id=0, has_side_effects=True),
    )(decay_rate, skip, lengths, inputs, dt, b_proj, c_proj, grad_out)
    if not fused:
        gb = lax.psum_scatter(gb, "head", scatter_dimension=0, tiled=True)
        gc = lax.psum_scatter(gc, "head", scatter_dimension=0, tiled=True)
    results = (mixed, gx, gdt, gb, gc)
    hbm = pl.BlockSpec(memory_space=pltpu.VMEM)
    return pl.pallas_call(
        move,
        out_shape=tuple(jax.ShapeDtypeStruct(r.shape, r.dtype) for r in results),
        in_specs=[hbm] * 5,
        out_specs=(hbm,) * 5,
    )(*results)


def solution(mesh):
    return jax.shard_map(
        functools.partial(per_device, mesh.shape["ctx"], mesh.shape["head"]),
        mesh=mesh,
        in_specs=(
            P("head", None, "ctx"),
            P("head", "ctx"),
            P("head"),
            P("head"),
            P(None, "ctx"),
            P(None, "ctx"),
            P(),
            P("head", None, "ctx"),
        ),
        out_specs=(
            P("head", None, "ctx"),
            P("head", None, "ctx"),
            P("head", "ctx"),
            P("head", "ctx"),
            P("head", "ctx"),
        ),
        check_vma=False,
    )
```

```python
import functools
import jax
import jax.numpy as jnp
from jax import lax
from jax.experimental import pallas as pl
from jax.experimental.pallas import tpu as pltpu
from jax.sharding import PartitionSpec as P

Q = 128
HIGH = lax.Precision.HIGHEST
F32 = jnp.float32
BF16 = jnp.bfloat16
MESH = pl.DeviceIdType.MESH


def mm(a, b, ca, cb):
    return lax.dot_general(a, b, (((ca,), (cb,)), ((), ())), preferred_element_type=F32)


def split(v):
    hi = v.astype(BF16)
    return hi, (v - hi.astype(F32)).astype(BF16)


def lanes(a, b):
    return jnp.concatenate([a, b], axis=1)


def rows(a, b):
    return jnp.concatenate([a, b], axis=0)


def kernel(cfg, rate_ref, skip_ref, len_ref, x_ref, dt_ref, b_ref, c_ref, g_ref, *refs):
    n_ctx, n_head, hops, fused, ndoc = cfg
    mixed_ref, gx_ref, gdt_ref, gb_ref, gc_ref = refs[:5]
    (s_ref, gz_ref, ddt_ref, out_s, out_g, in_s, in_g, ctx_send, ctx_recv) = refs[5:14]
    if fused:
        part, recv1, send2, recv2, s1_send, s1_recv, s2_send, s2_recv = refs[14:]
    width_p = x_ref.shape[1]
    local = x_ref.shape[2]
    width_n = b_ref.shape[0]
    blocks = local // Q
    me = lax.axis_index("ctx")
    head = lax.axis_index("head")
    chips = n_head // 2
    core = lax.rem(head, 2)
    chip = head // 2

    barrier = pltpu.get_barrier_semaphore()

    @pl.when(me > 0)
    def _():
        pl.semaphore_signal(barrier, inc=1, device_id={"ctx": me - 1}, device_id_type=MESH)

    @pl.when(me < n_ctx - 1)
    def _():
        pl.semaphore_signal(barrier, inc=1, device_id={"ctx": me + 1}, device_id_type=MESH)

    if fused:
        pl.semaphore_signal(
            barrier, inc=1, device_id={"head": chip * 2 + 1 - core}, device_id_type=MESH
        )
        for d in range(1, chips):
            to = lax.rem(chip + d, chips) * 2 + core
            pl.semaphore_signal(barrier, inc=1, device_id={"head": to}, device_id_type=MESH)

    rate = rate_ref[0]
    skip = skip_ref[0]
    offset = me * local

    ends = []
    total = len_ref[0]
    for j in range(ndoc - 1):
        ends.append(total)
        total = total + len_ref[j + 1]

    def segment_of(pos):
        seg = jnp.zeros(pos.shape, jnp.int32)
        for end in ends:
            seg = seg + (pos >= end).astype(jnp.int32)
        return seg

    pos8 = (
        offset
        + lax.broadcasted_iota(jnp.int32, (blocks, Q), 0) * Q
        + lax.broadcasted_iota(jnp.int32, (blocks, Q), 1)
    )
    pos_t = (
        offset
        + lax.broadcasted_iota(jnp.int32, (Q, blocks), 1) * Q
        + lax.broadcasted_iota(jnp.int32, (Q, blocks), 0)
    )
    seg8 = segment_of(pos8)
    seg_t = segment_of(pos_t)
    before8 = jnp.where(pos8 == 0, -1, segment_of(pos8 - 1))
    prev8 = before8[:, 0:1]
    last8 = seg8[:, Q - 1 : Q]

    dt8 = jnp.concatenate([dt_ref[0:1, k * Q : (k + 1) * Q] for k in range(blocks)], axis=0)
    row_i = lax.broadcasted_iota(jnp.int32, (Q, Q), 0)
    col_j = lax.broadcasted_iota(jnp.int32, (Q, Q), 1)
    lower = row_i >= col_j
    lower_ones = lower.astype(F32)
    log8 = -rate * dt8
    cum8 = lax.dot_general(
        log8, lower_ones, (((1,), (1,)), ((), ())), precision=HIGH, preferred_element_type=F32
    )
    cum_t = lax.dot_general(
        lower_ones, log8, (((1,), (1,)), ((), ())), precision=HIGH, preferred_element_type=F32
    )
    end8 = cum8[:, Q - 1 : Q]
    din8 = jnp.where(seg8 == prev8, jnp.exp(cum8), 0.0)
    wdt8 = jnp.where(seg8 == last8, jnp.exp(end8 - cum8), 0.0) * dt8
    dall8 = jnp.where(last8 == prev8, jnp.exp(end8), 0.0)

    def cut(ref, k):
        return ref[0, :, k * Q : (k + 1) * Q]

    def cut2(ref, k):
        return ref[:, k * Q : (k + 1) * Q]

    state = jnp.zeros((width_p, width_n), F32)
    for k in range(blocks):
        s_ref[k] = state
        b_k = cut2(b_ref, k)
        hi, lo = split(cut(x_ref, k).astype(F32) * wdt8[k : k + 1])
        state = dall8[k : k + 1] * state + mm(lanes(hi, lo), lanes(b_k, b_k), 1, 1)
    out_s[0] = state
    carry = jnp.zeros((width_p, width_n), F32)
    for k in reversed(range(blocks)):
        gz_ref[k] = carry
        c_k = cut2(c_ref, k)
        hi, lo = split(cut(g_ref, k).astype(F32) * din8[k : k + 1])
        carry = dall8[k : k + 1] * carry + mm(lanes(hi, lo), lanes(c_k, c_k), 1, 1)
    out_g[0] = carry

    ahead = [None] * blocks
    prod = jnp.ones((1, 1), F32)
    for k in range(blocks):
        ahead[k] = prod
        prod = prod * dall8[k : k + 1]
    decay_dev = prod
    behind = [None] * blocks
    prod = jnp.ones((1, 1), F32)
    for k in reversed(range(blocks)):
        behind[k] = prod
        prod = prod * dall8[k : k + 1]

    @pl.when(me == 0)
    def _():
        in_s[...] = jnp.zeros_like(in_s)

    @pl.when(me == n_ctx - 1)
    def _():
        in_g[...] = jnp.zeros_like(in_g)

    peers = chips if fused else 0
    at_end = (me == 0) | (me == n_ctx - 1)

    @pl.when(at_end)
    def _():
        pl.semaphore_wait(barrier, peers + 1)

    @pl.when(jnp.logical_not(at_end))
    def _():
        pl.semaphore_wait(barrier, peers + 2)

    def ctx_copy(r, way):
        src, dst = (out_s, in_s) if way == 0 else (out_g, in_g)
        return pltpu.make_async_remote_copy(
            src_ref=src.at[r],
            dst_ref=dst.at[r],
            send_sem=ctx_send.at[r, way],
            recv_sem=ctx_recv.at[r, way],
            device_id={"ctx": me + 1 if way == 0 else me - 1},
            device_id_type=MESH,
        )

    def ctx_start(r):
        @pl.when(me < n_ctx - 1)
        def _():
            ctx_copy(r, 0).start()

        @pl.when(me > 0)
        def _():
            ctx_copy(r, 1).start()

    def ctx_wait(r):
        @pl.when(me > 0)
        def _():
            ctx_copy(r, 0).wait_recv()

        @pl.when(me < n_ctx - 1)
        def _():
            ctx_copy(r, 1).wait_recv()

    def ctx_done(r):
        @pl.when(me < n_ctx - 1)
        def _():
            ctx_copy(r, 0).wait_send()

        @pl.when(me > 0)
        def _():
            ctx_copy(r, 1).wait_send()

    ctx_start(0)

    def put(k, way, value, add):
        if fused:
            each = width_n // n_head
            chunk, lo = k // 2, (k % 2) * Q
            for h in range(n_head):
                at = (chunk, h % 2, h // 2, slice(way * each, (way + 1) * each), slice(lo, lo + Q))
                piece = value[h * each : (h + 1) * each]
                part[at] = part[at] + piece if add else piece
        else:
            ref = (gb_ref, gc_ref)[way]
            at = (slice(None), slice(k * Q, (k + 1) * Q))
            ref[at] = ref[at] + value if add else value

    def intra_w(k):
        x_k, g_k, b_k, c_k = cut(x_ref, k), cut(g_ref, k), cut2(b_ref, k), cut2(c_ref, k)
        mask = lower & (seg_t[:, k : k + 1] == seg8[k : k + 1])
        gap = jnp.where(mask, cum_t[:, k : k + 1] - cum8[k : k + 1], 0.0)
        ddt = jnp.where(mask, jnp.exp(gap), 0.0) * dt8[k : k + 1]
        ddt_ref[k] = ddt
        w_hi, w_lo = split(mm(g_k, x_k, 0, 0) * ddt)
        put(k, 0, mm(lanes(c_k, c_k), rows(w_hi, w_lo), 1, 0), False)
        put(k, 1, mm(lanes(b_k, b_k), lanes(w_hi, w_lo), 1, 1), False)

    diffs, qs, tails = [None] * blocks, [None] * blocks, [None] * blocks

    def inter_w(k, state_in, grad_in):
        x_k, g_k = cut(x_ref, k), cut(g_ref, k)
        s_k = s_ref[k] + ahead[k] * state_in
        gz = gz_ref[k] + behind[k] * grad_in
        s_ref[k] = s_k
        gz_ref[k] = gz
        s_hi, s_lo = split(s_k)
        z_hi, z_lo = split(gz)
        put(k, 0, mm(rows(z_hi, z_lo), rows(x_k, x_k), 0, 0) * wdt8[k : k + 1], True)
        put(k, 1, mm(rows(s_hi, s_lo), rows(g_k, g_k), 0, 0) * din8[k : k + 1], True)

    def outer(k, state_in):
        x_k, g_k, b_k, c_k = cut(x_ref, k), cut(g_ref, k), cut2(b_ref, k), cut2(c_ref, k)
        s_k = s_ref[k]
        gz = gz_ref[k]
        s_end = s_ref[k + 1] if k + 1 < blocks else out_s[0] + decay_dev * state_in
        tails[k] = jnp.sum(jnp.sum(gz * s_end, axis=0, keepdims=True), axis=1, keepdims=True)
        a_hi, a_lo = split(mm(c_k, b_k, 0, 0) * ddt_ref[k])
        s_hi, s_lo = split(s_k)
        z_hi, z_lo = split(gz)
        din, wdt = din8[k : k + 1], wdt8[k : k + 1]
        y = mm(lanes(x_k, x_k), lanes(a_hi, a_lo), 1, 1)
        y = y + mm(lanes(s_hi, s_lo), rows(c_k, c_k), 1, 0) * din
        v = mm(lanes(g_k, g_k), rows(a_hi, a_lo), 1, 0)
        v = v + mm(lanes(z_hi, z_lo), rows(b_k, b_k), 1, 0) * wdt
        x_f, g_f = x_k.astype(F32), g_k.astype(F32)
        mixed_ref[0, :, k * Q : (k + 1) * Q] = (y + skip * x_f).astype(BF16)
        gx_ref[0, :, k * Q : (k + 1) * Q] = (v + skip * g_f).astype(BF16)
        q_k = jnp.sum(x_f * v, axis=0, keepdims=True)
        qs[k] = q_k
        diffs[k] = jnp.sum(g_f * y, axis=0, keepdims=True) - q_k

    def pair_copy(chunk):
        return pltpu.make_async_remote_copy(
            src_ref=part.at[chunk, 1 - core],
            dst_ref=recv1.at[chunk],
            send_sem=s1_send.at[chunk],
            recv_sem=s1_recv.at[chunk],
            device_id={"head": chip * 2 + 1 - core},
            device_id_type=MESH,
        )

    def chip_copy(chunk, d):
        to = lax.rem(chip + d, chips)
        return pltpu.make_async_remote_copy(
            src_ref=send2.at[chunk, to],
            dst_ref=recv2.at[chunk, d - 1],
            send_sem=s2_send.at[chunk, d - 1],
            recv_sem=s2_recv.at[chunk, d - 1],
            device_id={"head": to * 2 + core},
            device_id_type=MESH,
        )

    def second(chunk):
        pair_copy(chunk).wait_recv()
        send2[chunk] = part[chunk, core] + recv1[chunk]
        for d in list(range(1, chips, 2)) + list(range(2, chips, 2)):
            chip_copy(chunk, d).start()

    for k in range(blocks):
        intra_w(k)
    ctx_wait(0)
    for r in range(1, hops):
        out_s[r] = out_s[0] + decay_dev * in_s[r - 1]
        out_g[r] = out_g[0] + decay_dev * in_g[r - 1]
        ctx_start(r)
        ctx_wait(r)
    state_in = in_s[hops - 1]
    grad_in = in_g[hops - 1]
    for k in range(blocks):
        inter_w(k, state_in, grad_in)
        if fused and k % 2 == 1:
            pair_copy(k // 2).start()
    for k in range(blocks):
        if fused and k < blocks // 2:
            second(k)
        outer(k, state_in)

    q8 = jnp.concatenate(qs, axis=0)
    r8 = jnp.concatenate(diffs, axis=0)
    tail8 = jnp.concatenate(tails, axis=0)
    back8 = lax.dot_general(
        r8, lower_ones, (((1,), (0,)), ((), ())), precision=HIGH, preferred_element_type=F32
    )
    gdt8 = q8 / dt8 - rate * (back8 + tail8)
    for k in range(blocks):
        gdt_ref[0:1, k * Q : (k + 1) * Q] = gdt8[k : k + 1]

    for r in range(hops):
        ctx_done(r)
    if fused:
        each = width_n // n_head
        chunks = blocks // 2
        for chunk in range(chunks):
            total = send2[chunk, chip]
            for d in range(1, chips):
                chip_copy(chunk, d).wait_recv()
                total = total + recv2[chunk, d - 1]
            at = slice(chunk * 2 * Q, (chunk + 1) * 2 * Q)
            gb_ref[:, at] = total[:each]
            gc_ref[:, at] = total[each:]
        for chunk in range(chunks):
            pair_copy(chunk).wait_send()
            for d in range(1, chips):
                chip_copy(chunk, d).wait_send()


def move(*refs):
    count = len(refs) // 2
    for i in range(count):
        refs[count + i][...] = refs[i][...]


def per_device(n_ctx, n_head, inputs, dt, decay_rate, skip, b_proj, c_proj, lengths, grad_out):
    _, width_p, local = inputs.shape
    width_n = b_proj.shape[0]
    longest = n_ctx * local // 4
    hops = max(1, min(n_ctx - 1, (longest - 2) // local + 1))
    each = width_n // n_head
    fused = each % 8 == 0
    blocks = local // Q
    chips = n_head // 2
    chunks = blocks // 2
    vmem = pl.BlockSpec(memory_space=pltpu.VMEM)
    smem = pl.BlockSpec(memory_space=pltpu.SMEM)
    grad_rows = each if fused else width_n
    scratch = [
        pltpu.VMEM((blocks, width_p, width_n), F32),
        pltpu.VMEM((blocks, width_p, width_n), F32),
        pltpu.VMEM((blocks, Q, Q), F32),
        pltpu.VMEM((hops, width_p, width_n), F32),
        pltpu.VMEM((hops, width_p, width_n), F32),
        pltpu.VMEM((hops, width_p, width_n), F32),
        pltpu.VMEM((hops, width_p, width_n), F32),
        pltpu.SemaphoreType.DMA((hops, 2)),
        pltpu.SemaphoreType.DMA((hops, 2)),
    ]
    if fused:
        scratch += [
            pltpu.VMEM((chunks, 2, chips, 2 * each, 2 * Q), F32),
            pltpu.VMEM((chunks, chips, 2 * each, 2 * Q), F32),
            pltpu.VMEM((chunks, chips, 2 * each, 2 * Q), F32),
            pltpu.VMEM((chunks, chips - 1, 2 * each, 2 * Q), F32),
            pltpu.SemaphoreType.DMA((chunks,)),
            pltpu.SemaphoreType.DMA((chunks,)),
            pltpu.SemaphoreType.DMA((chunks, chips - 1)),
            pltpu.SemaphoreType.DMA((chunks, chips - 1)),
        ]
    mixed, gx, gdt, gb, gc = pl.pallas_call(
        functools.partial(kernel, (n_ctx, n_head, hops, fused, lengths.shape[0])),
        out_shape=(
            jax.ShapeDtypeStruct(inputs.shape, BF16),
            jax.ShapeDtypeStruct(inputs.shape, BF16),
            jax.ShapeDtypeStruct(dt.shape, F32),
            jax.ShapeDtypeStruct((grad_rows, local), F32),
            jax.ShapeDtypeStruct((grad_rows, local), F32),
        ),
        in_specs=[smem, smem, smem, vmem, vmem, vmem, vmem, vmem],
        out_specs=(vmem,) * 5,
        scratch_shapes=scratch,
        compiler_params=pltpu.CompilerParams(collective_id=0, has_side_effects=True),
    )(decay_rate, skip, lengths, inputs, dt, b_proj, c_proj, grad_out)
    if not fused:
        gb = lax.psum_scatter(gb, "head", scatter_dimension=0, tiled=True)
        gc = lax.psum_scatter(gc, "head", scatter_dimension=0, tiled=True)
    results = (mixed, gx, gdt, gb, gc)
    hbm = pl.BlockSpec(memory_space=pltpu.VMEM)
    return pl.pallas_call(
        move,
        out_shape=tuple(jax.ShapeDtypeStruct(r.shape, r.dtype) for r in results),
        in_specs=[hbm] * 5,
        out_specs=(hbm,) * 5,
    )(*results)


def solution(mesh):
    return jax.shard_map(
        functools.partial(per_device, mesh.shape["ctx"], mesh.shape["head"]),
        mesh=mesh,
        in_specs=(
            P("head", None, "ctx"),
            P("head", "ctx"),
            P("head"),
            P("head"),
            P(None, "ctx"),
            P(None, "ctx"),
            P(),
            P("head", None, "ctx"),
        ),
        out_specs=(
            P("head", None, "ctx"),
            P("head", None, "ctx"),
            P("head", "ctx"),
            P("head", "ctx"),
            P("head", "ctx"),
        ),
        check_vma=False,
    )
```
